32 devices in a mesh: group: 4 (over z), dev: 8 (over y, x, core).
Axes of the slice: x: 2, y: 2, z: 4, core: 2. Of those that a mesh axis runs over, the one named last changes fastest.
Arguments:
- acts: bfloat16 [12288, 768], P(('group', 'dev')), may hold values from -6 to 6
- grad_out: bfloat16 [12288, 2048], P(('group', 'dev')), may hold values from -0.25 to 0.25
- live_rows: int32 [32], P(('group', 'dev')), may hold values from 96 to 384, as said below
- placement: int32 [32], replicated, may hold values from 0 to 7, as said below
- master: float32 [8, 768, 2048], P('group', 'dev'), may hold values from -0.21875 to 0.21875
- moment1: float32 [8, 768, 2048], P('group', 'dev'), may hold values from -3 to 3
- moment2: float32 [8, 768, 2048], P('group', 'dev'), may hold values from 0.05 to 5
Outputs:
- grad_in: bfloat16 [12288, 768], P(('group', 'dev'))
- new_master: float32 [8, 768, 2048], P('group', 'dev')
- new_moment1: float32 [8, 768, 2048], P('group', 'dev')
- new_moment2: float32 [8, 768, 2048], P('group', 'dev')
The draws below stay inside these ranges and needn't reach their ends.
Inputs may be any that keep to these rules, and one draw needn't show every extreme that they name: `placement`: every expert is named by some device. In each copy group (devices g * 8 to g * 8 + 7), for every index o of group exactly 2 devices run an expert e with e // 2 = o, and they all run the same one. `live_rows`: some device has all 384 slots live.
All inputs are finite; a program needn't handle non-finite values.
Results may differ from the reference program's by a relative error of at most 0.0085.
Values may be sent and summed in bfloat16 or wider, within the bound.
No kernel may reach another device: no remote copies, remote signals or barrier semaphores. Data moves between devices by JAX's collectives and lax.ppermute only.
A program may use at most 64 MiB of HBM per device.

```python
import math
import jax
import jax.numpy as jnp
from jax import lax

D = 2048
FF = 768
EXP_GROUP = 2
ROWS = 384
EXPERTS = 8
TOTAL_ROWS = 12288
N_GROUP = 4
N_DEV = 8
DEVICES = 32


def draw_placement(key, part):
    subkeys = jax.random.split(jax.random.fold_in(key, 11), 3)
    heavy = jax.random.randint(subkeys[0], (N_GROUP,), 1, N_GROUP)
    owner_keys = jax.random.split(subkeys[1], N_GROUP)
    orders = jax.vmap(lambda k: jax.random.permutation(k, N_GROUP))(owner_keys)
    picks = (orders < heavy[:, None]).astype(jnp.int32)
    group_keys = jax.random.split(subkeys[2], N_GROUP)
    slots = jax.vmap(lambda k: jax.random.permutation(k, N_DEV))(group_keys)
    owners = (slots % N_GROUP).astype(jnp.int32)
    chosen = picks.T
    bits = jnp.take_along_axis(chosen, owners, axis=1)
    experts = EXP_GROUP * owners + bits
    return experts.reshape(DEVICES).astype(jnp.int32)


def draw_live_rows(key, part):
    subkeys = jax.random.split(jax.random.fold_in(key, 23), 2)
    counts = jax.random.randint(subkeys[0], (DEVICES,), ROWS // 4, ROWS + 1)
    fullest = jax.random.randint(subkeys[1], (), 0, DEVICES)
    return counts.at[fullest].set(ROWS).astype(jnp.int32)


def steps_of(key, extent, shards, smallest, top_value):
    loudness, own = 1.0, jax.random.fold_in(key, 6)
    for axis_at, parts in shards:
        heights = jnp.exp(jax.random.uniform(jax.random.fold_in(own, axis_at), (parts,), jnp.float32, smallest / len(shards), top_value / len(shards)))
        loudness = loudness * jnp.repeat(heights, extent[axis_at] // parts).reshape([-1 if axis == axis_at else 1 for axis in range(len(extent))])
    return loudness


def centred(rng, extent, scale, bound, pieces=(), kind=jnp.bfloat16):
    entries = jax.random.normal(rng, extent, jnp.float32) * scale
    if len(pieces) > 0:
        entries = steps_of(rng, extent, pieces, -0.22, 0.18) * entries
    return jnp.clip(entries, min=-bound, max=bound).astype(kind)


def setup_inputs(seed: int = 0) -> dict:
    splits = jax.random.split(jax.random.key(seed), 8)
    acts = centred(splits[0], (TOTAL_ROWS, FF), 1.0, 6.0, ((0, 32),))
    grad_out = centred(splits[1], (TOTAL_ROWS, D), 0.04, 0.25, ((0, 32),))
    live_rows = draw_live_rows(jax.random.fold_in(splits[7], 71), 0)
    placement = draw_placement(jax.random.fold_in(splits[7], 71), 0)
    master = centred(splits[4], (EXPERTS, FF, D), FF ** -0.5, 0.21875, ((0, 4), (1, 8)), jnp.float32)
    moment1 = centred(splits[5], (EXPERTS, FF, D), 0.5, 3.0, ((0, 4), (1, 8)), jnp.float32)
    moment2 = jnp.clip(jnp.exp(math.log(5.0) - 4.6051702 * jax.random.uniform(splits[6], (EXPERTS, FF, D), jnp.float32) ** steps_of(splits[6], (EXPERTS, FF, D), ((0, 4), (1, 8)), -0.2, 0.2)), 0.05, 5.0)
    return dict(acts=acts, grad_out=grad_out, live_rows=live_rows, placement=placement, master=master, moment1=moment1, moment2=moment2)


beta_first = 0.9
beta_second = 0.95
learn_rate = 0.02
decay_rate = 0.1
epsilon = 1e-08
correct_first = 1.0 - (0.9 ** 50) ** 2
correct_second = 1.0 - (0.95 ** 50) ** 2

def reference(acts, grad_out, live_rows, placement, master, moment1, moment2):
    half_weights = master.astype(jnp.bfloat16)
    act_blocks = acts.reshape(N_GROUP, N_DEV, ROWS, FF)
    out_blocks = grad_out.reshape(N_GROUP, N_DEV, ROWS, D)
    live_blocks = live_rows.reshape(N_GROUP, N_DEV)
    place_blocks = placement.reshape(N_GROUP, N_DEV)
    positions = jnp.arange(ROWS, dtype=jnp.int32)

    def per_device(partial_value, inputs):
        act_rows, out_rows, live_count, expert = inputs
        weight = lax.dynamic_index_in_dim(half_weights, expert, 0, keepdims=False)
        live_mask = (positions < live_count)[:, None]
        grad_rows = jnp.dot(out_rows, weight.T, preferred_element_type=jnp.float32)
        grad_rows = jnp.where(live_mask, grad_rows, jnp.zeros((), grad_rows.dtype)).astype(jnp.bfloat16)
        masked = jnp.where(live_mask, act_rows, jnp.zeros((), act_rows.dtype))
        copy_grad = jnp.dot(masked.T, out_rows, preferred_element_type=jnp.float32).astype(jnp.bfloat16)
        copy_grad = lax.optimization_barrier(copy_grad).astype(jnp.float32)
        current = lax.dynamic_index_in_dim(partial_value, expert, 0, keepdims=False)
        partial_value = lax.dynamic_update_index_in_dim(partial_value, current + copy_grad, expert, 0)
        return (partial_value, grad_rows)

    def per_group(total, inputs):
        partial_value = jnp.zeros((EXPERTS, FF, D), jnp.float32)
        partial_value, grad_rows = lax.scan(per_device, partial_value, inputs)
        rounded = lax.optimization_barrier(partial_value.astype(jnp.bfloat16)).astype(jnp.float32)
        return (total + rounded, grad_rows)
    total = jnp.zeros((EXPERTS, FF, D), jnp.float32)
    gradient, grad_rows = lax.scan(per_group, total, (act_blocks, out_blocks, live_blocks, place_blocks))
    grad_in = grad_rows.reshape(N_GROUP * N_DEV * ROWS, FF)
    new_moment1 = beta_first * moment1 + (1.0 - beta_first) * gradient
    new_moment2 = beta_second * moment2 + (1.0 - beta_second) * gradient * gradient
    ascent = new_moment1 / correct_first / (jnp.sqrt(new_moment2 / correct_second) + epsilon)
    new_master = master - learn_rate * (ascent + decay_rate * master)
    return (grad_in, new_master, new_moment1, new_moment2)
```

```python
import functools

import jax
import jax.numpy as jnp
from jax import lax
from jax.experimental import pallas as pl
from jax.experimental.pallas import tpu as pltpu
from jax.sharding import PartitionSpec as P

beta_first = 0.9
beta_second = 0.95
learn_rate = 0.02
decay_rate = 0.1
epsilon = 1e-08
correct_first = 1.0 - (0.9**50) ** 2
correct_second = 1.0 - (0.95**50) ** 2


VMEM = pltpu.MemorySpace.VMEM
SMEM = pltpu.MemorySpace.SMEM
ANY = pl.ANY


def expert_of(place_ref, group, owner, dev_count, per_group):
    def step(w, found):
        e = place_ref[group * dev_count + w]
        return jnp.where(lax.div(e, per_group) == owner, e, found)

    return lax.fori_loop(0, dev_count, step, jnp.int32(0))


def pair_of(place_ref, group, owner, dev_count, per_group):
    def step(w, found):
        low, high = found
        hit = lax.div(place_ref[group * dev_count + w], per_group) == owner
        low = jnp.where(hit & (low < 0), w, low)
        high = jnp.where(hit, w, high)
        return low, high

    return lax.fori_loop(0, dev_count, step, (jnp.int32(-1), jnp.int32(0)))


def cast_kernel(dev_count, place_ref, master_ref, *outs):
    per_group = master_ref.shape[0]
    g = lax.axis_index("group")
    for t, out in enumerate(outs):
        e = expert_of(place_ref, lax.bitwise_xor(g, t), g, dev_count, per_group)
        out[...] = master_ref[e - g * per_group].astype(jnp.bfloat16)


def weight_grad_kernel(live_ref, acts_ref, go_ref, *refs):
    *outs, flipped, ordered = refs
    rows, ff = acts_ref.shape
    part = ff // len(outs)
    me = lax.axis_index("dev")

    @pl.when(pl.program_id(0) == 0)
    def _():
        alive = lax.broadcasted_iota(jnp.int32, (rows, 1), 0) < live_ref[0]
        acts = acts_ref[...].astype(jnp.float32)
        flipped[...] = jnp.where(alive, acts, 0.0).T.astype(jnp.bfloat16)
        for s in range(len(outs)):
            at = pl.multiple_of(lax.bitwise_xor(me, s) * part, 8)
            ordered[pl.ds(s * part, part), :] = flipped[pl.ds(at, part), :]

    block = jnp.dot(ordered[...], go_ref[...], preferred_element_type=jnp.float32)
    for s, out in enumerate(outs):
        out[...] = block[s * part : (s + 1) * part].astype(jnp.bfloat16)


def pair_sum_kernel(dev_count, per_group, group_count, place_ref, *refs):
    arrived = refs[:dev_count]
    outs = refs[dev_count : dev_count + group_count]
    held, sems = refs[dev_count + group_count :]
    g, me = lax.axis_index("group"), lax.axis_index("dev")
    copies = [
        pltpu.make_async_copy(r, held.at[s], sems.at[s]) for s, r in enumerate(arrived)
    ]
    for c in copies:
        c.start()
    for c in copies:
        c.wait()
    for t, out in enumerate(outs):
        low, high = pair_of(place_ref, g, lax.bitwise_xor(g, t), dev_count, per_group)
        first = held[lax.bitwise_xor(low, me)].astype(jnp.float32)
        second = held[lax.bitwise_xor(high, me)].astype(jnp.float32)
        out[...] = (first + second).astype(jnp.bfloat16)


def weight_pick_kernel(dev_count, per_group, group_count, place_ref, *refs):
    arrived = refs[:group_count]
    outs = refs[group_count : group_count + dev_count]
    held, in_sems, out_sems = refs[group_count + dev_count :]
    g, me = lax.axis_index("group"), lax.axis_index("dev")
    copies = [
        pltpu.make_async_copy(r, held.at[t], in_sems.at[t]) for t, r in enumerate(arrived)
    ]
    for c in copies:
        c.start()
    for c in copies:
        c.wait()
    copies = []
    for s, out in enumerate(outs):
        owner = lax.div(place_ref[g * dev_count + lax.bitwise_xor(me, s)], per_group)
        copies.append(
            pltpu.make_async_copy(
                held.at[lax.bitwise_xor(owner, g)], out, out_sems.at[s]
            )
        )
    for c in copies:
        c.start()
    for c in copies:
        c.wait()


def grad_in_kernel(tile, dev_count, live_ref, go_ref, *refs):
    arrived = refs[:dev_count]
    out_ref, weight, sems = refs[dev_count:]
    me = lax.axis_index("dev")
    ff = weight.shape[0]
    part = ff // dev_count
    copies = []
    for s, r in enumerate(arrived):
        at = pl.multiple_of(lax.bitwise_xor(me, s) * part, 8)
        copies.append(
            pltpu.make_async_copy(r, weight.at[pl.ds(at, part), :], sems.at[s])
        )
    for c in copies:
        c.start()
    for c in copies:
        c.wait()
    rows = go_ref.shape[0]
    alive = lax.broadcasted_iota(jnp.int32, (rows, 1), 0) < live_ref[0]
    for j in range(ff // tile):
        block = lax.dot_general(
            go_ref[...],
            weight[j * tile : (j + 1) * tile, :],
            (((1,), (1,)), ((), ())),
            preferred_element_type=jnp.float32,
        )
        out_ref[:, j * tile : (j + 1) * tile] = jnp.where(alive, block, 0.0).astype(
            jnp.bfloat16
        )


def adam_kernel(dev_count, per_group, group_count, place_ref, *refs):
    arrived = refs[:group_count]
    master_ref, moment1_ref, moment2_ref = refs[group_count : group_count + 3]
    new_master, new_moment1, new_moment2 = refs[-3:]
    g = lax.axis_index("group")
    j = pl.program_id(0)
    gradient = jnp.zeros(arrived[0].shape, jnp.float32)
    for t, r in enumerate(arrived):
        e = expert_of(place_ref, lax.bitwise_xor(g, t), g, dev_count, per_group)
        term = r[...].astype(jnp.float32)
        gradient += jnp.where(e - g * per_group == j, term, jnp.zeros_like(term))
    first = beta_first * moment1_ref[0] + (1.0 - beta_first) * gradient
    second = beta_second * moment2_ref[0] + (1.0 - beta_second) * gradient * gradient
    ascent = first / correct_first / (jnp.sqrt(second / correct_second) + epsilon)
    master = master_ref[0]
    new_master[0] = master - learn_rate * (ascent + decay_rate * master)
    new_moment1[0] = first
    new_moment2[0] = second


def exchange(blocks, axis, order):
    n = len(blocks)
    got = [blocks[0]] + [None] * (n - 1)
    for k in order:
        got[k] = lax.ppermute(blocks[k], axis, [(i, i ^ k) for i in range(n)])
    return got


def cost(flops, nbytes):
    return pl.CostEstimate(flops=flops, bytes_accessed=nbytes, transcendentals=0)


def on_device(chunks, acts, grad_out, live_rows, placement, master, moment1, moment2):
    dev_count = lax.axis_size("dev")
    group_count = lax.axis_size("group")
    rows, ff = acts.shape
    width = grad_out.shape[1]
    per_group, part = master.shape[0], master.shape[1]
    bf16, f32 = jnp.bfloat16, jnp.float32
    piece = width // chunks
    smem = pl.BlockSpec(memory_space=SMEM)
    vmem = pl.BlockSpec(memory_space=VMEM)
    anyspace = pl.BlockSpec(memory_space=ANY)
    group_order = [k for k in range(group_count // 2, group_count)]
    group_order += [k for k in range(1, group_count // 2)]
    dev_order = list(range(dev_count - 1, 0, -1))

    outgoing = pl.pallas_call(
        functools.partial(cast_kernel, dev_count),
        out_shape=[jax.ShapeDtypeStruct((part, width), bf16)] * group_count,
        in_specs=[smem, vmem],
        out_specs=[vmem] * group_count,
        cost_estimate=cost(part * width * group_count, 8 * part * width * group_count),
        name="cast_pick",
    )(placement, master)
    shards = exchange(outgoing, "group", group_order)

    tile = min(piece, 512)
    slots = []
    for c in range(chunks):
        blocks = pl.pallas_call(
            weight_grad_kernel,
            grid=(piece // tile,),
            out_shape=[jax.ShapeDtypeStruct((part, piece), bf16)] * dev_count,
            in_specs=[
                smem,
                pl.BlockSpec((rows, ff), lambda i: (0, 0)),
                pl.BlockSpec((rows, tile), lambda i, c=c: (0, c * (piece // tile) + i)),
            ],
            out_specs=[pl.BlockSpec((part, tile), lambda i: (0, i))] * dev_count,
            scratch_shapes=[pltpu.VMEM((ff, rows), bf16), pltpu.VMEM((ff, rows), bf16)],
            cost_estimate=cost(2 * rows * ff * piece, 2 * (rows + ff) * piece),
            name="weight_grad",
        )(live_rows, acts, grad_out)
        arrived = exchange(blocks, "dev", dev_order)
        sums = pl.pallas_call(
            functools.partial(pair_sum_kernel, dev_count, per_group, group_count),
            out_shape=[jax.ShapeDtypeStruct((part, piece), bf16)] * group_count,
            in_specs=[smem] + [anyspace] * dev_count,
            out_specs=[vmem] * group_count,
            scratch_shapes=[
                pltpu.VMEM((dev_count, part, piece), bf16),
                pltpu.SemaphoreType.DMA((dev_count,)),
            ],
            cost_estimate=cost(2 * ff * piece, 4 * ff * piece),
            name="pair_sum",
        )(placement, *arrived)
        slots.append(exchange(sums, "group", group_order))

    picked = pl.pallas_call(
        functools.partial(weight_pick_kernel, dev_count, per_group, group_count),
        out_shape=[jax.ShapeDtypeStruct((part, width), bf16)] * dev_count,
        in_specs=[smem] + [anyspace] * group_count,
        out_specs=[anyspace] * dev_count,
        scratch_shapes=[
            pltpu.VMEM((group_count, part, width), bf16),
            pltpu.SemaphoreType.DMA((group_count,)),
            pltpu.SemaphoreType.DMA((dev_count,)),
        ],
        cost_estimate=cost(0, 4 * ff * width),
        name="weight_pick",
    )(placement, *shards)
    weight = exchange(picked, "dev", dev_order)
    grad_in = pl.pallas_call(
        functools.partial(grad_in_kernel, 256, dev_count),
        out_shape=jax.ShapeDtypeStruct((rows, ff), bf16),
        in_specs=[smem, vmem] + [anyspace] * dev_count,
        out_specs=vmem,
        scratch_shapes=[
            pltpu.VMEM((ff, width), bf16),
            pltpu.SemaphoreType.DMA((dev_count,)),
        ],
        cost_estimate=cost(2 * rows * ff * width, 2 * (rows + ff) * width),
        name="grad_in",
    )(live_rows, grad_out, *weight)

    state = None
    for c in range(chunks):
        whole = pl.BlockSpec((1, part, piece), lambda j, c=c: (j, 0, c))
        prior = [] if state is None else list(state)
        state = pl.pallas_call(
            functools.partial(adam_kernel, dev_count, per_group, group_count),
            grid=(per_group,),
            out_shape=[jax.ShapeDtypeStruct(master.shape, f32)] * 3,
            in_specs=[smem]
            + [pl.BlockSpec((part, piece), lambda j: (0, 0))] * group_count
            + [whole] * 3
            + [anyspace] * len(prior),
            out_specs=[whole] * 3,
            input_output_aliases={1 + group_count + 3 + k: k for k in range(len(prior))},
            cost_estimate=cost(20 * per_group * part * piece, 26 * per_group * part * piece),
            name="adam",
        )(placement, *slots[c], master, moment1, moment2, *prior)
    new_master, new_moment1, new_moment2 = state
    return (grad_in, new_master, new_moment1, new_moment2)


def solution(mesh):
    in_specs = (
        P(("group", "dev"), None),
        P(("group", "dev"), None),
        P(("group", "dev")),
        P(),
        P("group", "dev", None),
        P("group", "dev", None),
        P("group", "dev", None),
    )
    out_specs = (
        P(("group", "dev"), None),
        P("group", "dev", None),
        P("group", "dev", None),
        P("group", "dev", None),
    )
    return jax.shard_map(
        functools.partial(on_device, 2),
        mesh=mesh,
        in_specs=in_specs,
        out_specs=out_specs,
        check_vma=False,
    )
```
